512 devices in a mesh: grp: 32 (over y_lo, z, core), blk: 16 (over x, y_hi).
Axes of the slice: x: 4, y: 8 (y_hi: 4, y_lo: 2; y = y_hi * 2 + y_lo), z: 8, core: 2. Of those that a mesh axis runs over, the one named last changes fastest.
Arguments:
- child_inverse: bfloat16 [32, 2, 2048, 2048], P('grp', None, 'blk'), may hold values from -0.09375 to 0.09375
- border_block: bfloat16 [32, 2, 2048, 2048], P('grp', None, 'blk'), may hold values from -0.09375 to 0.09375
- child_rhs: bfloat16 [32, 2, 2048, 256], P('grp', None, 'blk'), may hold values from -6 to 6
- parent_inverse: bfloat16 [32, 2, 4096, 2048], P('grp', None, 'blk'), may hold values from -0.0625 to 0.0625
- parent_rhs: bfloat16 [32, 2, 2048, 256], P('grp', None, 'blk'), may hold values from -6 to 6
- parent_of: int32 [32, 1], replicated, may hold values from 0 to 15
- owner: int32 [16], replicated, may hold values from 0 to 15, each once
- row_map: int32 [32, 2048], replicated, may hold values from 0 to 4095, as said below
Outputs:
- child_solution: bfloat16 [32, 2, 2048, 256], P('grp', None, 'blk')
- parent_solution: bfloat16 [32, 2, 2048, 256], P('grp', None, 'blk')
The draws below stay inside these ranges and needn't reach their ends.
Inputs may be any that keep to these rules, and one draw needn't show every extreme that they name: parent_of[c, 0] is the parent front of the sibling front on group c; every parent front has one sibling or more. owner[p] names the pair of groups 2 owner[p] and 2 owner[p] + 1 that holds parent front p; each pair holds one parent. row_map[c, j] differ for different j of one c; border row j with j // 128 = b goes to a parent row h * 2048 + b * 128 + r with h of 0 or 1 and r < 128.
All inputs are finite; a program needn't handle non-finite values.
Results may differ from the reference program's by a relative error of at most 0.008.
Values may be sent and summed in bfloat16 or wider, within the bound.
No kernel may reach another device: no remote copies, remote signals or barrier semaphores. Data moves between devices by JAX's collectives and lax.ppermute only.
A program may use at most 64 MiB of HBM per device.

```python
import jax
import jax.numpy as jnp
from jax import lax

PIV = 2048
BORDER = 2048
PPIV = 4096
SRC = 256
GROUPS = 32
PARENTS = 16
BROWS = 128
PROWS = 128


def draw_row_map(key, part):
    slices_count = BORDER // BROWS
    slot_total = GROUPS * slices_count
    slot_keys = jax.random.split(jax.random.fold_in(key, 7), slot_total)
    orders = jax.vmap(lambda single_key: jax.random.permutation(single_key, 2 * PROWS))(slot_keys)
    slot_ids = jnp.arange(slot_total)
    target_ids = jnp.where(slot_ids == 0, 0, jnp.where(slot_ids == slices_count - 1, 2 * PROWS - 1, -1))
    leading = orders[:, :1]
    orders = jnp.where(orders == target_ids[:, None], leading, orders)
    orders = orders.at[:, 0].set(jnp.where(target_ids >= 0, target_ids, orders[:, 0]))
    chosen = orders[:, :BROWS]
    half_index = chosen // PROWS
    offsets = chosen % PROWS
    block_index = (slot_ids % slices_count)[:, None]
    parent_row = half_index * (PPIV // 2) + block_index * PROWS + offsets
    return parent_row.reshape(GROUPS, BORDER).astype(jnp.int32)


def block_scale(key, extent, cuts, least, high):
    def one(dim, blocks):
        steps = jax.random.uniform(jax.random.fold_in(jax.random.fold_in(key, 6), dim), (blocks,), jnp.float32, least / len(cuts), high / len(cuts))
        return jnp.repeat(jnp.exp(steps), extent[dim] // blocks).reshape((-1,) + (1,) * (len(extent) - dim - 1))

    factor_of = one(*cuts[0])
    for cut in cuts[1:]:
        factor_of = factor_of * one(*cut)
    return factor_of


def picks_of(rng, rows, number_of, top, lift):
    ranking = jax.random.permutation(jax.random.fold_in(rng, 1), number_of)
    pull = ranking
    for power in range(3):
        pull = pull * pull // number_of
    pull = pull * lift // number_of
    tickets = jax.random.randint(jax.random.fold_in(rng, 2), (rows, number_of), 0, 4096) + pull
    fixed_rows = jax.random.permutation(jax.random.fold_in(rng, 3), rows)[jnp.arange(number_of) % rows]
    tickets = jnp.where(jnp.arange(rows)[:, None] == fixed_rows[None, :], 1 << 14, tickets)
    merit = tickets * number_of + jnp.arange(number_of)
    return lax.top_k(merit.astype(jnp.int32), top)[1].astype(jnp.int32)


def normal_values(key, shape, width, bound, pieces=(), kind=jnp.bfloat16):
    values = width * jax.random.normal(key, shape, jnp.float32)
    if pieces:
        values = values * block_scale(key, shape, pieces, -0.22, 0.18)
    return jnp.clip(values, -bound, bound).astype(kind)


def setup_inputs(seed: int = 0) -> dict:
    key_of = jax.random.split(jax.random.key(seed), 9)
    child_inverse = normal_values(key_of[0], (GROUPS, 2, PIV, PIV), (2 * PIV) ** -0.5, 0.09375, ((0, 32), (2, 16)))
    border_block = normal_values(key_of[1], (GROUPS, 2, BORDER, PIV), (2 * PIV) ** -0.5, 0.09375, ((0, 32), (2, 16)))
    child_rhs = normal_values(key_of[2], (GROUPS, 2, PIV, SRC), 1.0, 6.0, ((0, 32), (2, 16)))
    parent_inverse = normal_values(key_of[3], (GROUPS, 2, PPIV, PPIV // 2), (2 * PPIV) ** -0.5, 0.0625, ((0, 32), (2, 16)))
    parent_rhs = normal_values(key_of[4], (GROUPS, 2, PPIV // 2, SRC), 1.0, 6.0, ((0, 32), (2, 16)))
    parent_of = picks_of(key_of[5], GROUPS, PARENTS, 1, 1024)
    owner = jax.random.permutation(key_of[6], PARENTS).astype(jnp.int32)
    row_map = draw_row_map(jax.random.fold_in(key_of[8], 71), 0)
    return {"child_inverse": child_inverse, "border_block": border_block, "child_rhs": child_rhs, "parent_inverse": parent_inverse, "parent_rhs": parent_rhs, "parent_of": parent_of, "owner": owner, "row_map": row_map}


def complex_product(left, right):
    real_part = jnp.dot(left[0], right[0], preferred_element_type=jnp.float32) - jnp.dot(left[1], right[1], preferred_element_type=jnp.float32)
    imag_part = jnp.dot(left[0], right[1], preferred_element_type=jnp.float32) + jnp.dot(left[1], right[0], preferred_element_type=jnp.float32)
    return jnp.stack([real_part, imag_part])


def reference(child_inverse, border_block, child_rhs, parent_inverse, parent_rhs, parent_of, owner, row_map):
    def solve_child(element):
        inverse_part, border_part, source_part = element
        solved = complex_product(inverse_part, source_part).astype(jnp.bfloat16)
        update_part = (-complex_product(border_part, solved)).astype(jnp.bfloat16)
        return solved, update_part

    child_solution, updates = lax.map(solve_child, (child_inverse, border_block, child_rhs))
    pair_of_child = owner[parent_of[:, 0]].astype(jnp.int32)

    def add_child(totals, element):
        update_part, pair_index, row_list = element
        front_rows = totals[pair_index]
        front_rows = front_rows.at[:, row_list, :].add(update_part.astype(jnp.float32))
        return totals.at[pair_index].set(front_rows), None

    zero_sums = jnp.zeros((PARENTS, 2, PPIV, SRC), jnp.float32)
    sums, unused = lax.scan(add_child, zero_sums, (updates, pair_of_child, row_map.astype(jnp.int32)))
    own_rhs = parent_rhs.reshape(PARENTS, 2, 2, PPIV // 2, SRC).transpose(0, 2, 1, 3, 4).reshape(PARENTS, 2, PPIV, SRC)
    right_side = (own_rhs.astype(jnp.float32) + sums).astype(jnp.bfloat16)
    inverse_halves = parent_inverse.reshape(PARENTS, 2, 2, PPIV, PPIV // 2)

    def solve_parent(element):
        halves, rhs_part = element
        full_inverse = jnp.concatenate([halves[0], halves[1]], axis=-1)
        return complex_product(full_inverse, rhs_part)

    solved_parent = lax.map(solve_parent, (inverse_halves, right_side))
    blocks_count = PPIV // (2 * PROWS)
    arranged = solved_parent.reshape(PARENTS, 2, blocks_count, 2, PROWS, SRC).transpose(0, 3, 1, 2, 4, 5)
    parent_solution = arranged.reshape(GROUPS, 2, PPIV // 2, SRC).astype(jnp.bfloat16)
    return child_solution, parent_solution
```

```python
import functools

import jax
import jax.numpy as jnp
from jax import lax
from jax.experimental import pallas as pl
from jax.experimental.pallas import tpu as pltpu
from jax.sharding import PartitionSpec as P

F32 = jnp.float32
BF16 = jnp.bfloat16
GROUPS = 32
SIDE = 4
CHUNKS = 1
VM = pl.BlockSpec(memory_space=pltpu.VMEM)
SM = pl.BlockSpec(memory_space=pltpu.SMEM)


def cost(flops, moved):
    return pl.CostEstimate(flops=flops, bytes_accessed=moved, transcendentals=0)


def products(m_ref, g_ref):
    rows, inner = m_ref.shape[1:]
    cols = g_ref.shape[-1]
    both = m_ref[...].reshape(2 * rows, inner)
    with_real = jnp.dot(both, g_ref[:, 0].reshape(inner, cols), preferred_element_type=F32)
    with_imag = jnp.dot(both, g_ref[:, 1].reshape(inner, cols), preferred_element_type=F32)
    return with_real[:rows] - with_imag[rows:], with_imag[:rows] + with_real[rows:]


def solve_kernel(m_ref, g_ref, o_ref):
    real, imag = products(m_ref, g_ref)
    o_ref[0] = real.astype(BF16)
    o_ref[1] = imag.astype(BF16)


def update_kernel(m_ref, g_ref, o_ref):
    parts = products(m_ref, g_ref)
    wide = jnp.concatenate([-part.T for part in parts], axis=0)
    o_ref[...] = wide.astype(BF16).reshape(o_ref.shape)


def partial_kernel(half_ref, m_ref, g_ref, kept_ref, given_ref, full_ref):
    rows = kept_ref.shape[1]
    for part, value in enumerate(products(m_ref, g_ref)):
        full_ref[part] = value
    half = half_ref[0]
    mine = pl.ds(pl.multiple_of(half * rows, rows), rows)
    other = pl.ds(pl.multiple_of((1 - half) * rows, rows), rows)
    kept_ref[...] = full_ref[:, mine, :]
    given_ref[...] = full_ref[:, other, :].astype(BF16)


def route_kernel(parent_ref, owner_ref, rows_ref, v_ref, o_ref, sums_ref):
    rows = v_ref.shape[2]
    sums_ref[...] = jnp.zeros_like(sums_ref)
    slots = lax.broadcasted_iota(jnp.int32, (2 * rows, rows), 0)
    for child in range(GROUPS):
        wanted = jnp.broadcast_to(rows_ref[child : child + 1, :], (2 * rows, rows))
        table = jnp.where(slots == wanted, 1.0, 0.0).astype(BF16)
        placed = lax.dot_general(
            v_ref[child], table, (((1,), (1,)), ((), ())), preferred_element_type=F32
        )
        pair = owner_ref[parent_ref[child]]
        sums_ref[pair] += placed
    for pair in range(GROUPS // 2):
        for half in range(2):
            o_ref[2 * pair + half] = sums_ref[pair, :, half * rows : (half + 1) * rows].astype(BF16)


def right_kernel(b_ref, p_ref, o_ref):
    cols = p_ref.shape[2]
    flat = b_ref[...].reshape(2 * cols, b_ref.shape[2]).astype(F32)
    for part in range(2):
        o_ref[part] = (
            p_ref[part].astype(F32) + flat[part * cols : (part + 1) * cols].T
        ).astype(BF16)


def solve(matrix, gathered):
    rows, inner = matrix.shape[1:]
    cols = gathered.shape[-1]
    return pl.pallas_call(
        solve_kernel,
        out_shape=jax.ShapeDtypeStruct((2, rows, cols), BF16),
        in_specs=[VM, VM],
        out_specs=VM,
        cost_estimate=cost(8 * rows * inner * cols, 4 * inner * (rows + cols)),
    )(matrix, gathered)


def updates(matrix, gathered):
    rows, inner = matrix.shape[1:]
    cols = gathered.shape[-1]
    return pl.pallas_call(
        update_kernel,
        out_shape=jax.ShapeDtypeStruct((GROUPS, 2 * cols // GROUPS, rows), BF16),
        in_specs=[VM, VM],
        out_specs=VM,
        cost_estimate=cost(8 * rows * inner * cols, 4 * inner * (rows + cols)),
    )(matrix, gathered)


def partial(half, matrix, gathered):
    rows, inner = matrix.shape[1:]
    cols = gathered.shape[-1]
    return pl.pallas_call(
        partial_kernel,
        out_shape=(
            jax.ShapeDtypeStruct((2, rows // 2, cols), F32),
            jax.ShapeDtypeStruct((2, rows // 2, cols), BF16),
        ),
        in_specs=[SM, VM, VM],
        out_specs=(VM, VM),
        scratch_shapes=[pltpu.VMEM((2, rows, cols), F32)],
        cost_estimate=cost(8 * rows * inner * cols, 4 * inner * (rows + cols)),
    )(half, matrix, gathered)


def route(parent_of, owner, rows_of, pieces):
    width, rows = pieces.shape[1:]
    return pl.pallas_call(
        route_kernel,
        out_shape=jax.ShapeDtypeStruct(pieces.shape, BF16),
        in_specs=[SM, SM, VM, VM],
        out_specs=VM,
        scratch_shapes=[pltpu.VMEM((GROUPS // 2, width, 2 * rows), F32)],
        cost_estimate=cost(4 * GROUPS * width * rows * rows, 4 * GROUPS * width * rows),
    )(parent_of, owner, rows_of, pieces)


def right_side(back, parent_rhs):
    return pl.pallas_call(
        right_kernel,
        out_shape=jax.ShapeDtypeStruct(parent_rhs.shape, BF16),
        in_specs=[VM, VM],
        out_specs=VM,
        cost_estimate=cost(2 * parent_rhs.size, 6 * parent_rhs.size),
    )(back, parent_rhs)


def fanned(block, groups):
    copies = jnp.broadcast_to(block[None], (len(groups[0]),) + block.shape)
    return lax.all_to_all(copies, "blk", 0, 0, axis_index_groups=groups, tiled=True)


def gathered(block):
    along_y = [[i * SIDE + j for j in range(SIDE)] for i in range(SIDE)]
    along_x = [[i * SIDE + j for i in range(SIDE)] for j in range(SIDE)]
    whole = fanned(fanned(block, along_y), along_x)
    return whole.reshape((SIDE * SIDE,) + block.shape)


def exchanged(pieces):
    return lax.all_to_all(pieces, "grp", 0, 0, tiled=True)


def per_device(
    child_inverse, border_block, child_rhs, parent_inverse, parent_rhs, parent_of, owner, row_map
):
    slot_index = lax.axis_index("blk")
    half = jnp.reshape(lax.axis_index("grp") % 2, (1,)).astype(jnp.int32)
    rows, cols = child_rhs.shape[2:]
    local_map = lax.dynamic_slice_in_dim(row_map, slot_index * rows, rows, 1)
    half_order = 16 * rows
    rows_of = (local_map // half_order) * rows + local_map % rows
    parents = parent_of[:, 0]
    width = cols // CHUNKS

    solutions, answers = [], []
    for chunk in range(CHUNKS):
        here = slice(chunk * width, (chunk + 1) * width)
        solved = solve(child_inverse[0], gathered(child_rhs[0][:, :, here]))
        pieces = updates(border_block[0], gathered(solved))
        sums = exchanged(route(parents, owner, rows_of, exchanged(pieces)))
        right = right_side(sums, parent_rhs[0][:, :, here])
        kept, given = partial(half, parent_inverse[0], gathered(right))
        taken = lax.ppermute(given, "grp", [(i, i ^ 1) for i in range(GROUPS)])
        solutions.append(solved)
        answers.append((kept + taken.astype(F32)).astype(BF16))
    if CHUNKS == 1:
        return solutions[0][None], answers[0][None]
    return jnp.concatenate(solutions, -1)[None], jnp.concatenate(answers, -1)[None]


def solution(mesh):
    spec = P("grp", None, "blk", None)
    return jax.shard_map(
        per_device,
        mesh=mesh,
        in_specs=(spec,) * 5 + (P(), P(), P()),
        out_specs=(spec, spec),
        check_vma=False,
    )
```

```python
import jax
import jax.numpy as jnp
from jax import lax
from jax.experimental import pallas as pl
from jax.experimental.pallas import tpu as pltpu
from jax.sharding import PartitionSpec as P

F32 = jnp.float32
BF16 = jnp.bfloat16
GROUPS = 32
SIDE = 4
LIMIT = 12 << 20
VM = pl.BlockSpec(memory_space=pltpu.VMEM)
SM = pl.BlockSpec(memory_space=pltpu.SMEM)


def cost(flops, moved):
    return pl.CostEstimate(flops=flops, bytes_accessed=moved, transcendentals=0)


def products(m_ref, g_ref):
    rows, inner = m_ref.shape[1:]
    cols = g_ref.shape[-1]
    both = m_ref[...].reshape(2 * rows, inner)
    with_real = jnp.dot(both, g_ref[:, 0].reshape(inner, cols), preferred_element_type=F32)
    with_imag = jnp.dot(both, g_ref[:, 1].reshape(inner, cols), preferred_element_type=F32)
    return with_real[:rows] - with_imag[rows:], with_imag[:rows] + with_real[rows:]


def split_kernel(x_ref, m_ref, *o_refs):
    inner = o_refs[0].shape[2]
    for shift, o_ref in enumerate(o_refs):
        first = lax.rem(x_ref[0] + shift, SIDE) * inner
        o_ref[...] = m_ref[:, :, pl.ds(pl.multiple_of(first, inner), inner)]


def child_kernel(x_ref, *refs):
    *m_refs, g_ref, o_ref = refs
    for shift, m_ref in enumerate(m_refs):
        block = lax.rem(x_ref[0] + SIDE - shift, SIDE)
        for part, value in enumerate(products(m_ref, g_ref)):
            o_ref[block, part] = value.astype(BF16)


def parent_kernel(x_ref, *refs):
    *m_refs, g_ref, o_ref = refs
    rows = o_ref.shape[2]
    for shift, m_ref in enumerate(m_refs):
        block = lax.rem(x_ref[0] + SIDE - shift, SIDE)
        for part, value in enumerate(products(m_ref, g_ref)):
            for half in range(2):
                here = value[half * rows : (half + 1) * rows]
                o_ref[half * SIDE + block, part] = here.astype(BF16)


def total(p_ref, part):
    value = p_ref[0, part].astype(F32)
    for block in range(1, p_ref.shape[0]):
        value += p_ref[block, part].astype(F32)
    return value


def solved_kernel(p_ref, o_ref, fan_ref):
    for part in range(2):
        value = total(p_ref, part).astype(BF16)
        o_ref[part] = value
        for block in range(SIDE):
            fan_ref[block, part] = value


def pieces_kernel(p_ref, o_ref):
    wide = jnp.concatenate([-total(p_ref, part).T for part in range(2)], axis=0)
    o_ref[...] = wide.astype(BF16).reshape(o_ref.shape)


def answer_kernel(p_ref, o_ref):
    for part in range(2):
        o_ref[part] = total(p_ref, part).astype(BF16)


def route_kernel(parent_ref, owner_ref, rows_ref, v_ref, o_ref, sums_ref):
    rows = v_ref.shape[2]
    sums_ref[...] = jnp.zeros_like(sums_ref)
    slots = lax.broadcasted_iota(jnp.int32, (2 * rows, rows), 0)
    for child in range(GROUPS):
        wanted = jnp.broadcast_to(rows_ref[child : child + 1, :], (2 * rows, rows))
        table = jnp.where(slots == wanted, 1.0, 0.0).astype(BF16)
        placed = lax.dot_general(
            v_ref[child], table, (((1,), (1,)), ((), ())), preferred_element_type=F32
        )
        pair = owner_ref[parent_ref[child]]
        sums_ref[pair] += placed
    for pair in range(GROUPS // 2):
        for half in range(2):
            o_ref[2 * pair + half] = sums_ref[pair, :, half * rows : (half + 1) * rows].astype(BF16)


def right_kernel(b_ref, p_ref, fan_ref):
    cols = p_ref.shape[2]
    flat = b_ref[...].reshape(2 * cols, b_ref.shape[2]).astype(F32)
    for part in range(2):
        value = p_ref[part].astype(F32) + flat[part * cols : (part + 1) * cols].T
        for block in range(SIDE):
            fan_ref[block, part] = value.astype(BF16)


def local(kernel, outs, flops, *operands, scalars=0):
    moved = sum(x.size * x.dtype.itemsize for x in operands)
    shapes = [jax.ShapeDtypeStruct(shape, BF16) for shape in outs]
    return pl.pallas_call(
        kernel,
        out_shape=shapes if len(shapes) > 1 else shapes[0],
        in_specs=[SM] * scalars + [VM] * (len(operands) - scalars),
        out_specs=[VM] * len(shapes) if len(shapes) > 1 else VM,
        cost_estimate=cost(flops, moved + 2 * sum(x.size for x in shapes)),
        compiler_params=pltpu.CompilerParams(vmem_limit_bytes=LIMIT),
    )(*operands)


def route(parent_of, owner, rows_of, pieces):
    width, rows = pieces.shape[1:]
    return pl.pallas_call(
        route_kernel,
        out_shape=jax.ShapeDtypeStruct(pieces.shape, BF16),
        in_specs=[SM, SM, VM, VM],
        out_specs=VM,
        scratch_shapes=[pltpu.VMEM((GROUPS // 2, width, 2 * rows), F32)],
        cost_estimate=cost(4 * GROUPS * width * rows * rows, 4 * GROUPS * width * rows),
        compiler_params=pltpu.CompilerParams(vmem_limit_bytes=LIMIT),
    )(parent_of, owner, rows_of, pieces)


ALONG_Y = [[i * SIDE + j for j in range(SIDE)] for i in range(SIDE)]
ALONG_X = [[i * SIDE + j for i in range(SIDE)] for j in range(SIDE)]
ALONG_X_AND_CORE = [
    [(2 * pair + half) * SIDE * SIDE + i * SIDE + j for half in range(2) for i in range(SIDE)]
    for pair in range(GROUPS // 2)
    for j in range(SIDE)
]


def over(blocks, axis, groups=None):
    return lax.all_to_all(blocks, axis, 0, 0, axis_index_groups=groups, tiled=True)


def shifted(block, shift):
    pairs = [
        (i * SIDE + j, (i + shift) % SIDE * SIDE + j) for i in range(SIDE) for j in range(SIDE)
    ]
    return lax.ppermute(block, "blk", pairs)


def redistributed(here, matrix):
    rows, inner = matrix.shape[1:]
    blocks = local(split_kernel, [(2, rows, inner // SIDE)] * SIDE, 0, here, matrix, scalars=1)
    return [blocks[0]] + [shifted(blocks[shift], shift) for shift in range(1, SIDE)]


def per_device(
    child_inverse, border_block, child_rhs, parent_inverse, parent_rhs, parent_of, owner, row_map
):
    slot_index = lax.axis_index("blk")
    rows, cols = child_rhs.shape[2:]
    block = (2, rows, cols)
    fan = (SIDE,) + block
    flops = 8 * rows * cols * child_inverse.shape[3]
    local_map = lax.dynamic_slice_in_dim(row_map, slot_index * rows, rows, 1)
    half_order = SIDE * SIDE * rows
    rows_of = (local_map // half_order) * rows + local_map % rows

    here = jnp.reshape(slot_index // SIDE, (1,)).astype(jnp.int32)
    inverse = redistributed(here, child_inverse[0])
    border = redistributed(here, border_block[0])
    parent = redistributed(here, parent_inverse[0])

    source = over(jnp.broadcast_to(child_rhs[0][None], fan), "blk", ALONG_Y)
    parts = local(child_kernel, [fan], flops, here, *inverse, source, scalars=1)
    parts = over(parts, "blk", ALONG_X)
    solved, copies = local(solved_kernel, [block, fan], 0, parts)
    source = over(copies, "blk", ALONG_Y)
    parts = local(child_kernel, [fan], flops, here, *border, source, scalars=1)
    parts = over(parts, "blk", ALONG_X)
    pieces = local(pieces_kernel, [(GROUPS, 2 * cols // GROUPS, rows)], 0, parts)
    own, ahead, across, behind = parent
    columns, across = lax.optimization_barrier((over(pieces, "grp"), across))
    sums = over(route(parent_of[:, 0], owner, rows_of, columns), "grp")
    sums, ahead = lax.optimization_barrier((sums, ahead))
    parent = [own, ahead, across, behind]
    copies = local(right_kernel, [fan], 0, sums, parent_rhs[0])
    source = over(copies, "blk", ALONG_Y)
    parts = local(
        parent_kernel, [(2 * SIDE,) + block], 2 * flops, here, *parent, source, scalars=1
    )
    parts = over(parts, ("grp", "blk"), ALONG_X_AND_CORE)
    answer = local(answer_kernel, [block], 0, parts)
    return solved[None], answer[None]


def solution(mesh):
    spec = P("grp", None, "blk", None)
    return jax.shard_map(
        per_device,
        mesh=mesh,
        in_specs=(spec,) * 5 + (P(), P(), P()),
        out_specs=(spec, spec),
        check_vma=False,
    )
```

```python
import functools

import jax
import jax.numpy as jnp
from jax import lax
from jax.experimental import pallas as pl
from jax.experimental.pallas import tpu as pltpu
from jax.sharding import PartitionSpec as P


F32 = jnp.float32
BF16 = jnp.bfloat16
GROUPS = 32
SIDE = 4
LIMIT = 12 << 20
VM = pl.BlockSpec(memory_space=pltpu.VMEM)
SM = pl.BlockSpec(memory_space=pltpu.SMEM)


def cost(flops, moved):
    return pl.CostEstimate(flops=flops, bytes_accessed=moved, transcendentals=0)


def products(matrix, g_ref):
    rows, inner = matrix.shape[1:]
    cols = g_ref.shape[-1]
    both = matrix.reshape(2 * rows, inner)
    with_real = jnp.dot(both, g_ref[:, 0].reshape(inner, cols), preferred_element_type=F32)
    with_imag = jnp.dot(both, g_ref[:, 1].reshape(inner, cols), preferred_element_type=F32)
    return with_real[:rows] - with_imag[rows:], with_imag[:rows] + with_real[rows:]


def slice_kernel(x_ref, *refs):
    *m_refs, o_ref = refs
    for which, m_ref in enumerate(m_refs):
        o_ref[which] = m_ref[...]


def child_kernel(which, x_ref, *refs):
    *m_refs, g_ref, o_ref = refs
    for shift, m_ref in enumerate(m_refs):
        block = lax.rem(x_ref[0] + SIDE - shift, SIDE)
        for part, value in enumerate(products(m_ref[which], g_ref)):
            o_ref[block, part] = value.astype(BF16)


def parent_kernel(x_ref, *refs):
    *m_refs, g_ref, kept_ref, given_ref = refs
    rows = kept_ref.shape[2]
    half = x_ref[1]
    for shift, m_ref in enumerate(m_refs):
        block = lax.rem(x_ref[0] + SIDE - shift, SIDE)
        for part, value in enumerate(products(m_ref[0], g_ref)):
            top, low = value[:rows], value[rows:]
            kept_ref[block, part] = jnp.where(half == 0, top, low).astype(BF16)
            given_ref[block, part] = jnp.where(half == 0, low, top).astype(BF16)


def joined_kernel(a_ref, b_ref, o_ref):
    o_ref[...] = (a_ref[...].astype(F32) + b_ref[...].astype(F32)).astype(BF16)


def total(p_ref, part):
    value = p_ref[0, part].astype(F32)
    for block in range(1, p_ref.shape[0]):
        value += p_ref[block, part].astype(F32)
    return value


def pieces_kernel(p_ref, o_ref):
    wide = jnp.concatenate([-total(p_ref, part).T for part in range(2)], axis=0)
    o_ref[...] = wide.astype(BF16).reshape(o_ref.shape)


def total_kernel(p_ref, o_ref):
    for part in range(2):
        o_ref[part] = total(p_ref, part).astype(BF16)


def route_kernel(parent_ref, owner_ref, rows_ref, v_ref, o_ref, sums_ref):
    rows = v_ref.shape[2]
    sums_ref[...] = jnp.zeros_like(sums_ref)
    slots = lax.broadcasted_iota(jnp.int32, (2 * rows, rows), 0)
    for child in range(GROUPS):
        wanted = jnp.broadcast_to(rows_ref[child : child + 1, :], (2 * rows, rows))
        table = jnp.where(slots == wanted, 1.0, 0.0).astype(BF16)
        placed = lax.dot_general(
            v_ref[child], table, (((1,), (1,)), ((), ())), preferred_element_type=F32
        )
        pair = owner_ref[parent_ref[child]]
        sums_ref[pair] += placed
    for pair in range(GROUPS // 2):
        for half in range(2):
            o_ref[2 * pair + half] = sums_ref[pair, :, half * rows : (half + 1) * rows].astype(BF16)


def right_kernel(b_ref, p_ref, o_ref):
    cols = p_ref.shape[2]
    flat = b_ref[...].reshape(2 * cols, b_ref.shape[2]).astype(F32)
    for part in range(2):
        value = p_ref[part].astype(F32) + flat[part * cols : (part + 1) * cols].T
        o_ref[part] = value.astype(BF16)


def local(kernel, outs, flops, *operands, scalars=0):
    moved = sum(x.size * x.dtype.itemsize for x in operands)
    shapes = [jax.ShapeDtypeStruct(shape, BF16) for shape in outs]
    return pl.pallas_call(
        kernel,
        out_shape=shapes if len(shapes) > 1 else shapes[0],
        in_specs=[SM] * scalars + [VM] * (len(operands) - scalars),
        out_specs=[VM] * len(shapes) if len(shapes) > 1 else VM,
        cost_estimate=cost(flops, moved + 2 * sum(x.size for x in shapes)),
        compiler_params=pltpu.CompilerParams(vmem_limit_bytes=LIMIT),
    )(*operands)


def column_slice(here, shift, *matrices):
    rows, inner = matrices[0].shape[1:]
    shape = (2, rows, inner // SIDE)
    out = (len(matrices),) + shape
    return pl.pallas_call(
        slice_kernel,
        out_shape=jax.ShapeDtypeStruct(out, BF16),
        grid_spec=pltpu.PrefetchScalarGridSpec(
            num_scalar_prefetch=1,
            grid=(1,),
            in_specs=[
                pl.BlockSpec(shape, lambda i, x: (0, 0, lax.rem(x[0] + shift, SIDE)))
                for _ in matrices
            ],
            out_specs=pl.BlockSpec(out, lambda i, x: (0, 0, 0, 0)),
        ),
        cost_estimate=cost(0, 4 * len(matrices) * shape[0] * shape[1] * shape[2]),
        compiler_params=pltpu.CompilerParams(vmem_limit_bytes=LIMIT),
    )(here, *matrices)


def redistributed(here, *matrices):
    moved = [shifted(column_slice(here, k, *matrices), k) for k in range(1, SIDE)]
    return [column_slice(here, 0, *matrices)] + moved


def route(parent_of, owner, rows_of, pieces):
    width, rows = pieces.shape[1:]
    return pl.pallas_call(
        route_kernel,
        out_shape=jax.ShapeDtypeStruct(pieces.shape, BF16),
        in_specs=[SM, SM, VM, VM],
        out_specs=VM,
        scratch_shapes=[pltpu.VMEM((GROUPS // 2, width, 2 * rows), F32)],
        cost_estimate=cost(4 * GROUPS * width * rows * rows, 4 * GROUPS * width * rows),
        compiler_params=pltpu.CompilerParams(vmem_limit_bytes=LIMIT),
    )(parent_of, owner, rows_of, pieces)


ALONG_Y = [[i * SIDE + j for j in range(SIDE)] for i in range(SIDE)]
ALONG_X = [[i * SIDE + j for i in range(SIDE)] for j in range(SIDE)]


def over(blocks, axis, groups=None):
    return lax.all_to_all(blocks, axis, 0, 0, axis_index_groups=groups, tiled=True)


def shifted(block, shift):
    pairs = [
        (i * SIDE + j, (i + shift) % SIDE * SIDE + j) for i in range(SIDE) for j in range(SIDE)
    ]
    return lax.ppermute(block, "blk", pairs)


def along_y(block):
    return lax.all_gather(block, "blk", axis=0, tiled=False, axis_index_groups=ALONG_Y)


def along_x(blocks):
    return over(blocks, "blk", ALONG_X)


def per_device(
    child_inverse, border_block, child_rhs, parent_inverse, parent_rhs, parent_of, owner, row_map
):
    slot_index = lax.axis_index("blk")
    group_index = lax.axis_index("grp")
    rows, cols = child_rhs.shape[2:]
    block = (2, rows, cols)
    fan = (SIDE,) + block
    flops = 8 * rows * cols * child_inverse.shape[3]
    local_map = lax.dynamic_slice_in_dim(row_map, slot_index * rows, rows, 1)
    half_order = SIDE * SIDE * rows
    rows_of = (local_map // half_order) * rows + local_map % rows
    here = jnp.stack([slot_index // SIDE, group_index % 2]).astype(jnp.int32)

    child = redistributed(here, child_inverse[0], border_block[0])
    source = along_y(child_rhs[0])
    parts = local(functools.partial(child_kernel, 0), [fan], flops, here, *child, source, scalars=1)
    parts = along_x(parts)
    solved = local(total_kernel, [block], 0, parts)
    source = along_y(solved)
    parts = local(functools.partial(child_kernel, 1), [fan], flops, here, *child, source, scalars=1)
    parts = along_x(parts)
    pieces = local(pieces_kernel, [(GROUPS, 2 * cols // GROUPS, rows)], 0, parts)
    parent = redistributed(here, parent_inverse[0])
    columns = over(pieces, "grp")
    sums = route(parent_of[:, 0], owner, rows_of, columns)
    sums = over(sums, "grp")
    right = local(right_kernel, [block], 0, sums, parent_rhs[0])
    source = along_y(right)
    kept, given = local(parent_kernel, [fan, fan], 2 * flops, here, *parent, source, scalars=1)
    taken = lax.ppermute(given, "grp", [(i, i ^ 1) for i in range(GROUPS)])
    parts = local(joined_kernel, [fan], 0, kept, taken)
    parts = along_x(parts)
    answer = local(total_kernel, [block], 0, parts)
    return solved[None], answer[None]


def solution(mesh):
    spec = P("grp", None, "blk", None)
    return jax.shard_map(
        per_device,
        mesh=mesh,
        in_specs=(spec,) * 5 + (P(), P(), P()),
        out_specs=(spec, spec),
        check_vma=False,
    )
```

```python
import jax
import jax.numpy as jnp
from jax import lax
from jax.experimental import pallas as pl
from jax.experimental.pallas import tpu as pltpu
from jax.sharding import PartitionSpec as P


F32 = jnp.float32
BF16 = jnp.bfloat16
GROUPS = 32
SIDE = 4
LIMIT = 12 << 20
STEPS = 1
VM = pl.BlockSpec(memory_space=pltpu.VMEM)
SM = pl.BlockSpec(memory_space=pltpu.SMEM)


def cost(flops, moved):
    return pl.CostEstimate(flops=flops, bytes_accessed=moved, transcendentals=0)


def products(matrix, g_ref):
    rows, inner = matrix.shape[1:]
    cols = g_ref.shape[-1]
    both = matrix.reshape(2 * rows, inner)
    with_real = jnp.dot(both, g_ref[:, 0].reshape(inner, cols), preferred_element_type=F32)
    with_imag = jnp.dot(both, g_ref[:, 1].reshape(inner, cols), preferred_element_type=F32)
    return with_real[:rows] - with_imag[rows:], with_imag[:rows] + with_real[rows:]


def shift_kernel(x_ref, m_ref, *o_refs):
    inner = o_refs[0].shape[2]
    for shift, o_ref in enumerate(o_refs):
        first = lax.rem(x_ref[0] + shift, SIDE) * inner
        o_ref[...] = m_ref[:, :, pl.ds(pl.multiple_of(first, inner), inner)]


def split_kernel(m_ref, o_ref):
    inner = o_ref.shape[3]
    for block in range(SIDE):
        o_ref[block] = m_ref[:, :, block * inner : (block + 1) * inner]


def child_kernel(m_ref, g_ref, o_ref):
    for block in range(SIDE):
        for part, value in enumerate(products(m_ref[block], g_ref)):
            o_ref[block, part] = value.astype(BF16)


def parent_kernel(x_ref, *refs):
    *m_refs, g_ref, kept_ref, given_ref = refs
    rows = kept_ref.shape[2]
    half = x_ref[1]
    for shift, m_ref in enumerate(m_refs):
        block = lax.rem(x_ref[0] + SIDE - shift, SIDE)
        for part, value in enumerate(products(m_ref[...], g_ref)):
            top, low = value[:rows], value[rows:]
            kept_ref[block, part] = jnp.where(half == 0, top, low).astype(BF16)
            given_ref[block, part] = jnp.where(half == 0, low, top).astype(BF16)


def joined_kernel(a_ref, b_ref, o_ref):
    o_ref[...] = (a_ref[...].astype(F32) + b_ref[...].astype(F32)).astype(BF16)


def total(p_ref, part):
    value = p_ref[0, part].astype(F32)
    for block in range(1, p_ref.shape[0]):
        value += p_ref[block, part].astype(F32)
    return value


def pieces_kernel(p_ref, o_ref):
    wide = jnp.concatenate([-total(p_ref, part).T for part in range(2)], axis=0)
    o_ref[...] = wide.astype(BF16).reshape(o_ref.shape)


def total_kernel(p_ref, *o_refs):
    for part in range(2):
        value = total(p_ref, part).astype(BF16)
        for o_ref in o_refs:
            o_ref[part] = value


def route_kernel(parent_ref, owner_ref, rows_ref, v_ref, o_ref, sums_ref):
    rows = v_ref.shape[2]
    sums_ref[...] = jnp.zeros_like(sums_ref)
    slots = lax.broadcasted_iota(jnp.int32, (2 * rows, rows), 0)
    for child in range(GROUPS):
        wanted = jnp.broadcast_to(rows_ref[child : child + 1, :], (2 * rows, rows))
        table = jnp.where(slots == wanted, 1.0, 0.0).astype(BF16)
        placed = lax.dot_general(
            v_ref[child], table, (((1,), (1,)), ((), ())), preferred_element_type=F32
        )
        pair = owner_ref[parent_ref[child]]
        sums_ref[pair] += placed
    for pair in range(GROUPS // 2):
        for half in range(2):
            o_ref[2 * pair + half] = sums_ref[pair, :, half * rows : (half + 1) * rows].astype(BF16)


def right_kernel(b_ref, p_ref, o_ref):
    cols = p_ref.shape[2]
    flat = b_ref[...].reshape(2 * cols, b_ref.shape[2]).astype(F32)
    for part in range(2):
        value = p_ref[part].astype(F32) + flat[part * cols : (part + 1) * cols].T
        o_ref[part] = value.astype(BF16)


def local(kernel, outs, flops, *operands, scalars=0):
    moved = sum(x.size * x.dtype.itemsize for x in operands)
    shapes = [jax.ShapeDtypeStruct(shape, BF16) for shape in outs]
    return pl.pallas_call(
        kernel,
        out_shape=shapes if len(shapes) > 1 else shapes[0],
        in_specs=[SM] * scalars + [VM] * (len(operands) - scalars),
        out_specs=[VM] * len(shapes) if len(shapes) > 1 else VM,
        cost_estimate=cost(flops, moved + 2 * sum(x.size for x in shapes)),
        compiler_params=pltpu.CompilerParams(vmem_limit_bytes=LIMIT),
    )(*operands)


def shifted_columns(here, matrix):
    rows, inner = matrix.shape[1:]
    step = rows // STEPS
    piece = (2, step, inner // SIDE)
    return pl.pallas_call(
        shift_kernel,
        out_shape=[jax.ShapeDtypeStruct((2, rows, inner // SIDE), BF16)] * SIDE,
        grid_spec=pltpu.PrefetchScalarGridSpec(
            num_scalar_prefetch=1,
            grid=(STEPS,),
            in_specs=[pl.BlockSpec((2, step, inner), lambda i, x: (0, i, 0))],
            out_specs=[pl.BlockSpec(piece, lambda i, x: (0, i, 0))] * SIDE,
        ),
        cost_estimate=cost(0, 8 * rows * inner),
    )(here, matrix)


def column_blocks(matrix):
    rows, inner = matrix.shape[1:]
    step = rows // STEPS
    return pl.pallas_call(
        split_kernel,
        out_shape=jax.ShapeDtypeStruct((SIDE, 2, rows, inner // SIDE), BF16),
        grid=(STEPS,),
        in_specs=[pl.BlockSpec((2, step, inner), lambda i: (0, i, 0))],
        out_specs=pl.BlockSpec((SIDE, 2, step, inner // SIDE), lambda i: (0, 0, i, 0)),
        cost_estimate=cost(0, 8 * rows * inner),
    )(matrix)


def route(parent_of, owner, rows_of, pieces):
    width, rows = pieces.shape[1:]
    return pl.pallas_call(
        route_kernel,
        out_shape=jax.ShapeDtypeStruct(pieces.shape, BF16),
        in_specs=[SM, SM, VM, VM],
        out_specs=VM,
        scratch_shapes=[pltpu.VMEM((GROUPS // 2, width, 2 * rows), F32)],
        cost_estimate=cost(4 * GROUPS * width * rows * rows, 4 * GROUPS * width * rows),
        compiler_params=pltpu.CompilerParams(vmem_limit_bytes=LIMIT),
    )(parent_of, owner, rows_of, pieces)


ALONG_Y = [[i * SIDE + j for j in range(SIDE)] for i in range(SIDE)]
ALONG_X = [[i * SIDE + j for i in range(SIDE)] for j in range(SIDE)]


def over(blocks, axis, groups=None):
    return lax.all_to_all(blocks, axis, 0, 0, axis_index_groups=groups, tiled=True)


def shifted(block, shift):
    pairs = [
        (i * SIDE + j, (i + shift) % SIDE * SIDE + j) for i in range(SIDE) for j in range(SIDE)
    ]
    return lax.ppermute(block, "blk", pairs)


def along_y(block):
    return lax.all_gather(block, "blk", axis=0, tiled=False, axis_index_groups=ALONG_Y)


def along_x(blocks):
    return over(blocks, "blk", ALONG_X)


def per_device(
    child_inverse, border_block, child_rhs, parent_inverse, parent_rhs, parent_of, owner, row_map
):
    slot_index = lax.axis_index("blk")
    group_index = lax.axis_index("grp")
    rows, cols = child_rhs.shape[2:]
    block = (2, rows, cols)
    fan = (SIDE,) + block
    flops = 8 * rows * cols * child_inverse.shape[3]
    local_map = lax.dynamic_slice_in_dim(row_map, slot_index * rows, rows, 1)
    half_order = SIDE * SIDE * rows
    rows_of = (local_map // half_order) * rows + local_map % rows
    here = jnp.stack([slot_index // SIDE, group_index % 2]).astype(jnp.int32)

    inverse = along_x(column_blocks(child_inverse[0]))
    source = along_y(child_rhs[0])
    parts = local(child_kernel, [fan], flops, inverse, source)
    parts = along_x(parts)
    solved, sent = local(total_kernel, [block] * 2, 0, parts)
    source = along_y(sent)
    border, solved = lax.optimization_barrier((column_blocks(border_block[0]), solved))
    border = along_x(border)
    parts = local(child_kernel, [fan], flops, border, source)
    parts = along_x(parts)
    parent = shifted_columns(here, parent_inverse[0])
    parts, *parent = lax.optimization_barrier((parts, *parent))
    pieces = local(pieces_kernel, [(GROUPS, 2 * cols // GROUPS, rows)], 0, parts)
    parent[2] = shifted(parent[2], 2)
    parent[1] = shifted(parent[1], 1)
    parent[3] = shifted(parent[3], 3)
    columns = over(pieces, "grp")
    sums = route(parent_of[:, 0], owner, rows_of, columns)
    sums = over(sums, "grp")
    right = local(right_kernel, [block], 0, sums, parent_rhs[0])
    source = along_y(right)
    kept, given = local(parent_kernel, [fan, fan], 2 * flops, here, *parent, source, scalars=1)
    taken = lax.ppermute(given, "grp", [(i, i ^ 1) for i in range(GROUPS)])
    parts = local(joined_kernel, [fan], 0, kept, taken)
    parts = along_x(parts)
    answer = local(total_kernel, [block], 0, parts)
    return solved[None], answer[None]


def solution(mesh):
    spec = P("grp", None, "blk", None)
    return jax.shard_map(
        per_device,
        mesh=mesh,
        in_specs=(spec,) * 5 + (P(), P(), P()),
        out_specs=(spec, spec),
        check_vma=False,
    )
```

```python
import functools

import jax
import jax.numpy as jnp
from jax import lax
from jax.experimental import pallas as pl
from jax.experimental.pallas import tpu as pltpu
from jax.sharding import PartitionSpec as P


F32 = jnp.float32
BF16 = jnp.bfloat16
GROUPS = 32
SIDE = 4
LIMIT = 12 << 20
STEPS = 1
VM = pl.BlockSpec(memory_space=pltpu.VMEM)
SM = pl.BlockSpec(memory_space=pltpu.SMEM)


def cost(flops, moved):
    return pl.CostEstimate(flops=flops, bytes_accessed=moved, transcendentals=0)


def products(matrix, g_ref):
    rows, inner = matrix.shape[1:]
    cols = g_ref.shape[-1]
    both = matrix.reshape(2 * rows, inner)
    with_real = jnp.dot(both, g_ref[:, 0].reshape(inner, cols), preferred_element_type=F32)
    with_imag = jnp.dot(both, g_ref[:, 1].reshape(inner, cols), preferred_element_type=F32)
    return with_real[:rows] - with_imag[rows:], with_imag[:rows] + with_real[rows:]


def shift_kernel(x_ref, m_ref, *o_refs):
    inner = o_refs[0].shape[2]
    for shift, o_ref in enumerate(o_refs):
        first = lax.rem(x_ref[0] + shift, SIDE) * inner
        o_ref[...] = m_ref[:, :, pl.ds(pl.multiple_of(first, inner), inner)]


def split_kernel(m_ref, o_ref):
    inner = o_ref.shape[3]
    for block in range(SIDE):
        o_ref[block] = m_ref[:, :, block * inner : (block + 1) * inner]


def child_kernel(m_ref, g_ref, o_ref):
    for block in range(SIDE):
        for part, value in enumerate(products(m_ref[block], g_ref)):
            o_ref[block, part] = value.astype(BF16)


def parent_kernel(own, x_ref, *refs):
    *m_refs, g_ref, o_ref = refs
    rows = o_ref.shape[2]
    half = x_ref[1] if own else 1 - x_ref[1]
    here = pl.ds(pl.multiple_of(half * rows, rows), rows)
    for shift, m_ref in enumerate(m_refs):
        block = lax.rem(x_ref[0] + SIDE - shift, SIDE)
        for part, value in enumerate(products(m_ref[:, here, :], g_ref)):
            o_ref[block, part] = value.astype(BF16)


def joined_kernel(a_ref, b_ref, o_ref):
    o_ref[...] = (a_ref[...].astype(F32) + b_ref[...].astype(F32)).astype(BF16)


def total(p_ref, part):
    value = p_ref[0, part].astype(F32)
    for block in range(1, p_ref.shape[0]):
        value += p_ref[block, part].astype(F32)
    return value


def pieces_kernel(p_ref, o_ref):
    wide = jnp.concatenate([-total(p_ref, part).T for part in range(2)], axis=0)
    o_ref[...] = wide.astype(BF16).reshape(o_ref.shape)


def total_kernel(p_ref, *o_refs):
    for part in range(2):
        value = total(p_ref, part).astype(BF16)
        for o_ref in o_refs:
            o_ref[part] = value


def route_kernel(parent_ref, owner_ref, rows_ref, v_ref, o_ref, sums_ref):
    rows = v_ref.shape[2]
    sums_ref[...] = jnp.zeros_like(sums_ref)
    slots = lax.broadcasted_iota(jnp.int32, (2 * rows, rows), 0)
    for child in range(GROUPS):
        wanted = jnp.broadcast_to(rows_ref[child : child + 1, :], (2 * rows, rows))
        table = jnp.where(slots == wanted, 1.0, 0.0).astype(BF16)
        placed = lax.dot_general(
            v_ref[child], table, (((1,), (1,)), ((), ())), preferred_element_type=F32
        )
        pair = owner_ref[parent_ref[child]]
        sums_ref[pair] += placed
    for pair in range(GROUPS // 2):
        for half in range(2):
            o_ref[2 * pair + half] = sums_ref[pair, :, half * rows : (half + 1) * rows].astype(BF16)


def right_kernel(b_ref, p_ref, o_ref):
    cols = p_ref.shape[2]
    flat = b_ref[...].reshape(2 * cols, b_ref.shape[2]).astype(F32)
    for part in range(2):
        value = p_ref[part].astype(F32) + flat[part * cols : (part + 1) * cols].T
        o_ref[part] = value.astype(BF16)


def local(kernel, outs, flops, *operands, scalars=0):
    moved = sum(x.size * x.dtype.itemsize for x in operands)
    shapes = [jax.ShapeDtypeStruct(shape, BF16) for shape in outs]
    return pl.pallas_call(
        kernel,
        out_shape=shapes if len(shapes) > 1 else shapes[0],
        in_specs=[SM] * scalars + [VM] * (len(operands) - scalars),
        out_specs=[VM] * len(shapes) if len(shapes) > 1 else VM,
        cost_estimate=cost(flops, moved + 2 * sum(x.size for x in shapes)),
        compiler_params=pltpu.CompilerParams(vmem_limit_bytes=LIMIT),
    )(*operands)


def shifted_columns(here, matrix):
    rows, inner = matrix.shape[1:]
    step = rows // STEPS
    piece = (2, step, inner // SIDE)
    return pl.pallas_call(
        shift_kernel,
        out_shape=[jax.ShapeDtypeStruct((2, rows, inner // SIDE), BF16)] * SIDE,
        grid_spec=pltpu.PrefetchScalarGridSpec(
            num_scalar_prefetch=1,
            grid=(STEPS,),
            in_specs=[pl.BlockSpec((2, step, inner), lambda i, x: (0, i, 0))],
            out_specs=[pl.BlockSpec(piece, lambda i, x: (0, i, 0))] * SIDE,
        ),
        cost_estimate=cost(0, 8 * rows * inner),
    )(here, matrix)


def column_blocks(matrix):
    rows, inner = matrix.shape[1:]
    step = rows // STEPS
    return pl.pallas_call(
        split_kernel,
        out_shape=jax.ShapeDtypeStruct((SIDE, 2, rows, inner // SIDE), BF16),
        grid=(STEPS,),
        in_specs=[pl.BlockSpec((2, step, inner), lambda i: (0, i, 0))],
        out_specs=pl.BlockSpec((SIDE, 2, step, inner // SIDE), lambda i: (0, 0, i, 0)),
        cost_estimate=cost(0, 8 * rows * inner),
    )(matrix)


def route(parent_of, owner, rows_of, pieces):
    width, rows = pieces.shape[1:]
    return pl.pallas_call(
        route_kernel,
        out_shape=jax.ShapeDtypeStruct(pieces.shape, BF16),
        in_specs=[SM, SM, VM, VM],
        out_specs=VM,
        scratch_shapes=[pltpu.VMEM((GROUPS // 2, width, 2 * rows), F32)],
        cost_estimate=cost(4 * GROUPS * width * rows * rows, 4 * GROUPS * width * rows),
        compiler_params=pltpu.CompilerParams(vmem_limit_bytes=LIMIT),
    )(parent_of, owner, rows_of, pieces)


ALONG_Y = [[i * SIDE + j for j in range(SIDE)] for i in range(SIDE)]
ALONG_X = [[i * SIDE + j for i in range(SIDE)] for j in range(SIDE)]


def over(blocks, axis, groups=None):
    return lax.all_to_all(blocks, axis, 0, 0, axis_index_groups=groups, tiled=True)


def shifted(block, shift):
    pairs = [
        (i * SIDE + j, (i + shift) % SIDE * SIDE + j) for i in range(SIDE) for j in range(SIDE)
    ]
    return lax.ppermute(block, "blk", pairs)


def along_y(block):
    return lax.all_gather(block, "blk", axis=0, tiled=False, axis_index_groups=ALONG_Y)


def along_x(blocks):
    return over(blocks, "blk", ALONG_X)


def per_device(
    child_inverse, border_block, child_rhs, parent_inverse, parent_rhs, parent_of, owner, row_map
):
    slot_index = lax.axis_index("blk")
    group_index = lax.axis_index("grp")
    rows, cols = child_rhs.shape[2:]
    block = (2, rows, cols)
    fan = (SIDE,) + block
    flops = 8 * rows * cols * child_inverse.shape[3]
    local_map = lax.dynamic_slice_in_dim(row_map, slot_index * rows, rows, 1)
    half_order = SIDE * SIDE * rows
    rows_of = (local_map // half_order) * rows + local_map % rows
    here = jnp.stack([slot_index // SIDE, group_index % 2]).astype(jnp.int32)

    inverse = along_x(column_blocks(child_inverse[0]))
    source = along_y(child_rhs[0])
    parts = local(child_kernel, [fan], flops, inverse, source)
    parts = along_x(parts)
    parent = shifted_columns(here, parent_inverse[0])
    parts, *parent = lax.optimization_barrier((parts, *parent))
    solved, sent = local(total_kernel, [block] * 2, 0, parts)
    source = along_y(sent)
    border, solved = lax.optimization_barrier((column_blocks(border_block[0]), solved))
    border = along_x(border)
    parts = local(child_kernel, [fan], flops, border, source)
    parts = along_x(parts)
    pieces = local(pieces_kernel, [(GROUPS, 2 * cols // GROUPS, rows)], 0, parts)
    parent[2] = shifted(parent[2], 2)
    parent[1] = shifted(parent[1], 1)
    parent[3] = shifted(parent[3], 3)
    columns = over(pieces, "grp")
    sums = route(parent_of[:, 0], owner, rows_of, columns)
    sums = over(sums, "grp")
    right = local(right_kernel, [block], 0, sums, parent_rhs[0])
    source = along_y(right)
    given, kept = (
        local(functools.partial(parent_kernel, own), [fan], flops, here, *parent, source, scalars=1)
        for own in (False, True)
    )
    taken = lax.ppermute(given, "grp", [(i, i ^ 1) for i in range(GROUPS)])
    parts = local(joined_kernel, [fan], 0, kept, taken)
    parts = along_x(parts)
    answer = local(total_kernel, [block], 0, parts)
    return solved[None], answer[None]


def solution(mesh):
    spec = P("grp", None, "blk", None)
    return jax.shard_map(
        per_device,
        mesh=mesh,
        in_specs=(spec,) * 5 + (P(), P(), P()),
        out_specs=(spec, spec),
        check_vma=False,
    )
```

```python
import functools

import jax
import jax.numpy as jnp
from jax import lax
from jax.experimental import pallas as pl
from jax.experimental.pallas import tpu as pltpu
from jax.sharding import PartitionSpec as P


F32 = jnp.float32
BF16 = jnp.bfloat16
GROUPS = 32
SIDE = 4
LIMIT = 12 << 20
VM = pl.BlockSpec(memory_space=pltpu.VMEM)
SM = pl.BlockSpec(memory_space=pltpu.SMEM)


def cost(flops, moved):
    return pl.CostEstimate(flops=flops, bytes_accessed=moved, transcendentals=0)


def products(matrix, g_ref):
    rows, inner = matrix.shape[1:]
    cols = g_ref.shape[-1]
    both = matrix.reshape(2 * rows, inner)
    with_real = jnp.dot(both, g_ref[:, 0].reshape(inner, cols), preferred_element_type=F32)
    with_imag = jnp.dot(both, g_ref[:, 1].reshape(inner, cols), preferred_element_type=F32)
    return with_real[:rows] - with_imag[rows:], with_imag[:rows] + with_real[rows:]


def shift_kernel(m_ref, *o_refs):
    inner = o_refs[0].shape[2]
    column = lax.axis_index("blk") // SIDE
    for shift, o_ref in enumerate(o_refs):
        first = lax.rem(column + shift, SIDE) * inner
        o_ref[...] = m_ref[:, :, pl.ds(pl.multiple_of(first, inner), inner)]


def split_kernel(m_ref, o_ref):
    inner = o_ref.shape[3]
    for block in range(SIDE):
        o_ref[block] = m_ref[:, :, block * inner : (block + 1) * inner]


def child_kernel(m_ref, g_ref, o_ref):
    for block in range(SIDE):
        for part, value in enumerate(products(m_ref[block], g_ref)):
            o_ref[block, part] = value.astype(BF16)


def parent_kernel(own, *refs):
    *m_refs, g_ref, o_ref = refs
    rows = o_ref.shape[2]
    column = lax.axis_index("blk") // SIDE
    half = lax.rem(lax.axis_index("grp") + (0 if own else 1), 2)
    here = pl.ds(pl.multiple_of(half * rows, rows), rows)
    for shift, m_ref in enumerate(m_refs):
        block = lax.rem(column + SIDE - shift, SIDE)
        for part, value in enumerate(products(m_ref[:, here, :], g_ref)):
            o_ref[block, part] = value.astype(BF16)


def joined_kernel(a_ref, b_ref, o_ref):
    o_ref[...] = (a_ref[...].astype(F32) + b_ref[...].astype(F32)).astype(BF16)


def total(p_ref, part):
    value = p_ref[0, part].astype(F32)
    for block in range(1, p_ref.shape[0]):
        value += p_ref[block, part].astype(F32)
    return value


def pieces_kernel(p_ref, o_ref):
    wide = jnp.concatenate([-total(p_ref, part).T for part in range(2)], axis=0)
    o_ref[...] = wide.astype(BF16).reshape(o_ref.shape)


def total_kernel(p_ref, *o_refs):
    for part in range(2):
        value = total(p_ref, part).astype(BF16)
        for o_ref in o_refs:
            o_ref[part] = value


def route_kernel(parent_ref, owner_ref, rows_ref, v_ref, o_ref, sums_ref):
    rows = v_ref.shape[2]
    sums_ref[...] = jnp.zeros_like(sums_ref)
    slots = lax.broadcasted_iota(jnp.int32, (2 * rows, rows), 0)
    for child in range(GROUPS):
        wanted = jnp.broadcast_to(rows_ref[child : child + 1, :], (2 * rows, rows))
        table = jnp.where(slots == wanted, 1.0, 0.0).astype(BF16)
        placed = lax.dot_general(
            v_ref[child], table, (((1,), (1,)), ((), ())), preferred_element_type=F32
        )
        pair = owner_ref[parent_ref[child]]
        sums_ref[pair] += placed
    for pair in range(GROUPS // 2):
        for half in range(2):
            o_ref[2 * pair + half] = sums_ref[pair, :, half * rows : (half + 1) * rows].astype(BF16)


def right_kernel(b_ref, p_ref, o_ref):
    cols = p_ref.shape[2]
    flat = b_ref[...].reshape(2 * cols, b_ref.shape[2]).astype(F32)
    for part in range(2):
        value = p_ref[part].astype(F32) + flat[part * cols : (part + 1) * cols].T
        o_ref[part] = value.astype(BF16)


def local(kernel, outs, flops, *operands):
    moved = sum(x.size * x.dtype.itemsize for x in operands)
    shapes = [jax.ShapeDtypeStruct(shape, BF16) for shape in outs]
    return pl.pallas_call(
        kernel,
        out_shape=shapes if len(shapes) > 1 else shapes[0],
        in_specs=[VM] * len(operands),
        out_specs=[VM] * len(shapes) if len(shapes) > 1 else VM,
        cost_estimate=cost(flops, moved + 2 * sum(x.size for x in shapes)),
        compiler_params=pltpu.CompilerParams(vmem_limit_bytes=LIMIT),
    )(*operands)


def shifted_columns(matrix):
    rows, inner = matrix.shape[1:]
    return pl.pallas_call(
        shift_kernel,
        out_shape=[jax.ShapeDtypeStruct((2, rows, inner // SIDE), BF16)] * SIDE,
        in_specs=[VM],
        out_specs=[VM] * SIDE,
        cost_estimate=cost(0, 8 * rows * inner),
    )(matrix)


def column_blocks(matrix):
    rows, inner = matrix.shape[1:]
    return pl.pallas_call(
        split_kernel,
        out_shape=jax.ShapeDtypeStruct((SIDE, 2, rows, inner // SIDE), BF16),
        grid=(2,),
        in_specs=[pl.BlockSpec((1, rows, inner), lambda i: (i, 0, 0))],
        out_specs=pl.BlockSpec((SIDE, 1, rows, inner // SIDE), lambda i: (0, i, 0, 0)),
        cost_estimate=cost(0, 8 * rows * inner),
    )(matrix)


def route(parent_of, owner, rows_of, pieces):
    width, rows = pieces.shape[1:]
    return pl.pallas_call(
        route_kernel,
        out_shape=jax.ShapeDtypeStruct(pieces.shape, BF16),
        in_specs=[SM, SM, VM, VM],
        out_specs=VM,
        scratch_shapes=[pltpu.VMEM((GROUPS // 2, width, 2 * rows), F32)],
        cost_estimate=cost(4 * GROUPS * width * rows * rows, 4 * GROUPS * width * rows),
        compiler_params=pltpu.CompilerParams(vmem_limit_bytes=LIMIT),
    )(parent_of, owner, rows_of, pieces)


ALONG_Y = [[i * SIDE + j for j in range(SIDE)] for i in range(SIDE)]
ALONG_X = [[i * SIDE + j for i in range(SIDE)] for j in range(SIDE)]


def over(blocks, axis, groups=None):
    return lax.all_to_all(blocks, axis, 0, 0, axis_index_groups=groups, tiled=True)


def shifted(block, shift):
    pairs = [
        (i * SIDE + j, (i + shift) % SIDE * SIDE + j) for i in range(SIDE) for j in range(SIDE)
    ]
    return lax.ppermute(block, "blk", pairs)


def along_y(block):
    return lax.all_gather(block, "blk", axis=0, tiled=False, axis_index_groups=ALONG_Y)


def along_x(blocks):
    return over(blocks, "blk", ALONG_X)


def per_device(
    child_inverse, border_block, child_rhs, parent_inverse, parent_rhs, parent_of, owner, row_map
):
    slot_index = lax.axis_index("blk")
    rows, cols = child_rhs.shape[2:]
    block = (2, rows, cols)
    fan = (SIDE,) + block
    flops = 8 * rows * cols * child_inverse.shape[3]
    local_map = lax.dynamic_slice_in_dim(row_map, slot_index * rows, rows, 1)
    half_order = SIDE * SIDE * rows
    rows_of = (local_map // half_order) * rows + local_map % rows

    inverse = along_x(column_blocks(child_inverse[0]))
    source = along_y(child_rhs[0])
    parts = local(child_kernel, [fan], flops, inverse, source)
    parts = along_x(parts)
    parent = shifted_columns(parent_inverse[0])
    parts, *parent = lax.optimization_barrier((parts, *parent))
    solved, sent = local(total_kernel, [block] * 2, 0, parts)
    source = along_y(sent)
    border, solved = lax.optimization_barrier((column_blocks(border_block[0]), solved))
    border = along_x(border)
    parts = local(child_kernel, [fan], flops, border, source)
    parts = along_x(parts)
    pieces = local(pieces_kernel, [(GROUPS, 2 * cols // GROUPS, rows)], 0, parts)
    parent[2] = shifted(parent[2], 2)
    parent[1] = shifted(parent[1], 1)
    parent[3] = shifted(parent[3], 3)
    columns = over(pieces, "grp")
    sums = route(parent_of[:, 0], owner, rows_of, columns)
    sums = over(sums, "grp")
    right = local(right_kernel, [block], 0, sums, parent_rhs[0])
    source = along_y(right)
    given, kept = (
        local(functools.partial(parent_kernel, own), [fan], flops, *parent, source)
        for own in (False, True)
    )
    taken = lax.ppermute(given, "grp", [(i, i ^ 1) for i in range(GROUPS)])
    parts = local(joined_kernel, [fan], 0, kept, taken)
    parts = along_x(parts)
    answer = local(total_kernel, [block], 0, parts)
    return solved[None], answer[None]


def solution(mesh):
    spec = P("grp", None, "blk", None)
    return jax.shard_map(
        per_device,
        mesh=mesh,
        in_specs=(spec,) * 5 + (P(), P(), P()),
        out_specs=(spec, spec),
        check_vma=False,
    )
```
